32 devices in a mesh: shot: 2 (over y), row: 4 (over x, core), freq: 4 (over z).
Axes of the slice: x: 2, y: 2, z: 4, core: 2. Of those that a mesh axis runs over, the one named last changes fastest.
Arguments:
- source_field: float32 [2, 8, 1024, 1024], P(None, ('shot', 'freq'), 'row'), parts along dimension 1, may hold values from -6 to 6
- receiver_field: float32 [2, 8, 1024, 1024], P(None, ('shot', 'freq'), 'row'), parts along dimension 1, may hold values from -6 to 6
- slowness: float32 [4, 1024, 1024], P('freq', 'row'), may hold values from 0.22 to 0.67
- owner: int32 [4], replicated, may hold values from 0 to 3, each once
- freq_index: int32 [8], P(('shot', 'freq')), parts along dimension 0, may hold values from 0 to 3, each once
Outputs:
- source_out: float32 [2, 8, 1024, 1024], P(None, ('shot', 'freq'), 'row'), parts along dimension 1
- receiver_out: float32 [2, 8, 1024, 1024], P(None, ('shot', 'freq'), 'row'), parts along dimension 1
- image: float32 [4, 1024, 1024], P('shot', 'row', 'freq'), parts along dimension 0
The draws below stay inside these ranges and needn't reach their ends.
There are 2 independent parts, one for each index of `shot`. The reference program is written for one: setup_inputs(seed, part) draws one part's arguments, and reference() takes and returns one part's arrays. A program takes and returns all parts, laid end to end along the dimension named above; an argument that names none is the same for every part. Nothing has to cross between parts.
All inputs are finite; a program needn't handle non-finite values.
Results may differ from the reference program's by a relative error of at most 0.00022.
Values sent between devices are 32-bit elements; how exact they have to be, the bound alone decides.
A program may use at most 128 MiB of HBM per device.

```python
import math
import jax
import jax.numpy as jnp
from jax import lax

NX = 1024
NY = 1024
NZ = 2
FREQS = 4
SLABS = 4


def level_of(own_key, dims, split, least, top_value):
    level, own = 1.0, jax.random.fold_in(own_key, 6)
    for position, blocks in split:
        heights = jnp.exp(jax.random.uniform(jax.random.fold_in(own, position), (blocks,), jnp.float32, least / len(split), top_value / len(split)))
        level = level * jnp.repeat(heights, dims[position] // blocks).reshape([-1 if axis == position else 1 for axis in range(len(dims))])
    return level


def centred(own_key, extent, scale, reach, split=(), kind=jnp.bfloat16):
    drawn = jax.random.normal(own_key, extent, jnp.float32) * scale
    if len(split) > 0:
        drawn = level_of(own_key, extent, split, -0.22, 0.18) * drawn
    return jnp.clip(drawn, min=-reach, max=reach).astype(kind)


def setup_inputs(seed: int = 0, part: int = 0) -> dict:
    seeds = jax.random.split(jax.random.key(seed), 6)
    part_keys = jax.random.split(jax.random.fold_in(seeds[5], part), 6)
    source_field = centred(part_keys[0], (2, FREQS, NX, NY), 1.0, 6.0, ((1, 4), (2, 4)), jnp.float32)
    receiver_field = centred(part_keys[1], (2, FREQS, NX, NY), 1.0, 6.0, ((1, 4), (2, 4)), jnp.float32)
    slowness = jnp.clip(0.22 + 0.45000002 * jax.random.uniform(seeds[2], (SLABS, NX, NY), jnp.float32) ** level_of(seeds[2], (SLABS, NX, NY), ((0, 4), (1, 4)), -0.2, 0.2), 0.22, 0.67)
    owner = jax.random.permutation(seeds[3], SLABS).astype(jnp.int32)
    freq_index = jax.random.permutation(part_keys[4], FREQS).astype(jnp.int32)
    return dict(source_field=source_field, receiver_field=receiver_field, slowness=slowness, owner=owner, freq_index=freq_index)


dz_km = 0.01
dx_km = 0.0125
ref_slow = 0.5
base_hertz = 3.0
step_hertz = 4.0
taper = 0.5


def wavenumbers(length):
    index = jnp.arange(length, dtype=jnp.int32)
    signed = jnp.where(index * 2 < length, index, index - length)
    return signed.astype(jnp.float32) * (2.0 * math.pi / (length * dx_km))


def reference(source_field, receiver_field, slowness, owner, freq_index):
    kx_all = wavenumbers(NX)
    ky_all = wavenumbers(NY)
    square = kx_all[:, None] ** 2 + ky_all[None, :] ** 2
    kmax = math.pi / dx_km
    damp = jnp.exp(-taper * square / (kmax * kmax))
    omega = 2.0 * math.pi * (base_hertz + step_hertz * freq_index.astype(jnp.float32))
    slabs = [slowness[owner[depth]] for depth in range(NZ)]

    def one_freq(packed):
        omega_one, src_re, src_im, rec_re, rec_im = packed
        source = src_re + 1j * src_im
        receiver = rec_re + 1j * rec_im
        ws0 = omega_one * ref_slow
        vertical = ws0 - 0.5 * square / ws0
        terms = []
        for depth in range(NZ):
            source = jnp.fft.ifft2(jnp.fft.fft2(source) * damp * jnp.exp(1j * dz_km * vertical))
            receiver = jnp.fft.ifft2(jnp.fft.fft2(receiver) * damp * jnp.exp(-1j * dz_km * vertical))
            theta = omega_one * (slabs[depth] - ref_slow) * dz_km
            source = source * jnp.exp(1j * theta)
            receiver = receiver * jnp.exp(-1j * theta)
            terms.append(jnp.real(source) * jnp.real(receiver) + jnp.imag(source) * jnp.imag(receiver))
        return (jnp.real(source), jnp.imag(source), jnp.real(receiver), jnp.imag(receiver), jnp.stack(terms))

    src_re, src_im, rec_re, rec_im, terms = lax.map(
        one_freq, (omega, source_field[0], source_field[1], receiver_field[0], receiver_field[1]))
    image = jnp.sum(terms, axis=0)
    return jnp.stack([src_re, src_im]), jnp.stack([rec_re, rec_im]), image
```

```python
import math

import jax
import jax.numpy as jnp
from jax import lax
from jax.experimental import pallas as pl
from jax.experimental.pallas import tpu as pltpu
from jax.sharding import PartitionSpec as P

dz_km = 0.01
dx_km = 0.0125
base_hertz = 3.0
step_hertz = 4.0
taper = 0.5
vmem_bytes = 56 * 1024 * 1024


def split_high_low(value):
    high = lax.reduce_precision(value, 8, 7)
    return high.astype(jnp.bfloat16), (value - high).astype(jnp.bfloat16)


def toeplitz_blocks(length, omega):
    quarter = length // 4
    place = jnp.arange(quarter, dtype=jnp.int32)
    kept = 4 * place[None, :] + jnp.arange(4, dtype=jnp.int32)[:, None]
    signed = jnp.where(kept * 2 < length, kept, kept - length)
    square = (signed.astype(jnp.float32) * (2.0 * math.pi / (length * dx_km))) ** 2
    kmax = math.pi / dx_km
    damp = jnp.exp(-taper * square / (kmax * kmax)) / float(length)
    phase = (-dz_km / omega) * square
    amp_r = (damp * jnp.cos(phase))[:, None, :]
    amp_i = (damp * jnp.sin(phase))[:, None, :]
    turns = (kept[:, None, :] * place[None, :, None] % length).astype(jnp.float32)
    turns = turns * (2.0 * math.pi / length)
    cos_v = jnp.cos(turns)
    sin_v = jnp.sin(turns)
    left = jnp.concatenate([cos_v * amp_r - sin_v * amp_i, sin_v * amp_r + cos_v * amp_i], axis=2)
    right = jnp.concatenate(
        [jnp.concatenate([cos_v, sin_v], axis=2), jnp.concatenate([-sin_v, cos_v], axis=2)], axis=1
    )
    both = jnp.einsum("kbm,kcm->kbc", left, right, precision=lax.Precision.HIGHEST)
    return both[:, :, :quarter], both[:, :, quarter:]


def pack(real, imag, sign):
    top = jnp.concatenate([real, -sign * imag], axis=2)
    low = jnp.concatenate([sign * imag, real], axis=2)
    return split_high_low(jnp.concatenate([top, low], axis=1))


def column_matrix(real, imag):
    return pack(real, imag, 1.0)


def row_matrix(real, imag):
    turned_r = jnp.stack([real[0], real[3], real[2], real[1]])
    turned_i = jnp.stack([imag[0], imag[3], imag[2], imag[1]])
    return pack(turned_r, turned_i, -1.0)


def butterfly(re, im, sign):
    sum_r, dif_r = re[0] + re[2], re[0] - re[2]
    sum_i, dif_i = im[0] + im[2], im[0] - im[2]
    odd_r, gap_r = re[1] + re[3], re[1] - re[3]
    odd_i, gap_i = im[1] + im[3], im[1] - im[3]
    if sign < 0:
        gap_r, gap_i = -gap_r, -gap_i
    out_r = [sum_r + odd_r, dif_r - gap_i, sum_r - odd_r, dif_r + gap_i]
    out_i = [sum_i + odd_i, dif_i + gap_r, sum_i - odd_i, dif_i - gap_r]
    return out_r, out_i


def halves(value):
    high = value.astype(jnp.bfloat16)
    return high, (value - high.astype(jnp.float32)).astype(jnp.bfloat16)


def dot(left, right):
    return jnp.dot(left, right, preferred_element_type=jnp.float32)


def filter_rows(re, im, high_ref, low_ref):
    quarter = re[0].shape[1]
    re, im = butterfly(re, im, -1)
    out_r, out_i = [], []
    for k in range(4):
        high, low = halves(jnp.concatenate([re[k], im[k]], axis=1))
        out = dot(high, high_ref[k]) + (dot(low, high_ref[k]) + dot(high, low_ref[k]))
        out_r.append(out[:, :quarter])
        out_i.append(out[:, quarter:])
    return butterfly(out_r, out_i, 1)


def filter_cols(re, im, high_ref, low_ref):
    quarter = re[0].shape[0]
    re, im = butterfly(re, im, -1)
    out_r, out_i = [], []
    for k in range(4):
        high, low = halves(jnp.concatenate([re[k], im[k]], axis=0))
        out = dot(high_ref[k], high) + (dot(high_ref[k], low) + dot(low_ref[k], high))
        out_r.append(out[:quarter])
        out_i.append(out[quarter:])
    return butterfly(out_r, out_i, 1)


def first_kernel(source_ref, receiver_ref, high_ref, low_ref, out_ref):
    rows = source_ref.shape[2]
    quarter = source_ref.shape[3] // 4
    re, im = [], []
    for j in range(4):
        span = pl.ds(j * quarter, quarter)
        re.append(jnp.concatenate([source_ref[0, 0, :, span], receiver_ref[0, 0, :, span]], axis=0))
        im.append(jnp.concatenate([source_ref[1, 0, :, span], -receiver_ref[1, 0, :, span]], axis=0))
    re, im = filter_rows(re, im, high_ref, low_ref)
    for j in range(4):
        out_ref[j, 0, 0] = re[j][:rows]
        out_ref[j, 0, 1] = im[j][:rows]
        out_ref[j, 1, 0] = re[j][rows:]
        out_ref[j, 1, 1] = im[j][rows:]


def middle_kernel(omega_ref, field_ref, slab_ref, high_ref, low_ref, out_ref, term_ref):
    cols = field_ref.shape[4]
    re = [jnp.concatenate([field_ref[j, 0, 0], field_ref[j, 1, 0]], axis=1) for j in range(4)]
    im = [jnp.concatenate([field_ref[j, 0, 1], field_ref[j, 1, 1]], axis=1) for j in range(4)]
    re, im = filter_cols(re, im, high_ref, low_ref)
    for j in range(4):
        theta = slab_ref[j] * (omega_ref[0] * dz_km)
        cos_v, sin_v = jnp.cos(theta), jnp.sin(theta)
        cos_v = jnp.concatenate([cos_v, cos_v], axis=1)
        sin_v = jnp.concatenate([sin_v, sin_v], axis=1)
        re[j], im[j] = re[j] * cos_v - im[j] * sin_v, im[j] * cos_v + re[j] * sin_v
        term_ref[j] = re[j][:, :cols] * re[j][:, cols:] - im[j][:, :cols] * im[j][:, cols:]
    re, im = filter_cols(re, im, high_ref, low_ref)
    for j in range(4):
        out_ref[j, 0, 0] = re[j][:, :cols]
        out_ref[j, 0, 1] = im[j][:, :cols]
        out_ref[j, 1, 0] = re[j][:, cols:]
        out_ref[j, 1, 1] = im[j][:, cols:]


def last_kernel(omega_ref, field_ref, slab_ref, high_ref, low_ref, source_ref, receiver_ref, term_ref):
    rows, quarter = field_ref.shape[3:]
    re = [jnp.concatenate([field_ref[j, 0, 0], field_ref[j, 1, 0]], axis=0) for j in range(4)]
    im = [jnp.concatenate([field_ref[j, 0, 1], field_ref[j, 1, 1]], axis=0) for j in range(4)]
    re, im = filter_rows(re, im, high_ref, low_ref)
    for j in range(4):
        span = pl.ds(j * quarter, quarter)
        theta = slab_ref[:, span] * (omega_ref[0] * dz_km)
        cos_v, sin_v = jnp.cos(theta), jnp.sin(theta)
        cos_v = jnp.concatenate([cos_v, cos_v], axis=0)
        sin_v = jnp.concatenate([sin_v, sin_v], axis=0)
        out_r, out_i = re[j] * cos_v - im[j] * sin_v, im[j] * cos_v + re[j] * sin_v
        term_ref[:, span] = out_r[:rows] * out_r[rows:] - out_i[:rows] * out_i[rows:]
        source_ref[0, 0, :, span] = out_r[:rows]
        source_ref[1, 0, :, span] = out_i[:rows]
        receiver_ref[0, 0, :, span] = out_r[rows:]
        receiver_ref[1, 0, :, span] = -out_i[rows:]


def params():
    return pltpu.CompilerParams(vmem_limit_bytes=vmem_bytes, dimension_semantics=("arbitrary",))


def whole(shape):
    return pl.BlockSpec(shape, lambda i: (0,) * len(shape))


scalar = pl.BlockSpec(memory_space=pltpu.SMEM)


def body(source_field, receiver_field, slowness, owner, freq_index):
    rows, width = source_field.shape[2:]
    row_count = lax.axis_size("row")
    freq_count = lax.axis_size("freq")
    height = rows * row_count
    cols = width // row_count
    quart_w = width // 4
    quart_h = height // 4
    omega = 2.0 * math.pi * (base_hertz + step_hertz * freq_index.astype(jnp.float32))
    slabs = lax.all_gather(slowness, "freq", axis=0, tiled=True)
    slab_first = lax.dynamic_index_in_dim(slabs, owner[0], 0, keepdims=False)
    slab_last = lax.dynamic_index_in_dim(slabs, owner[1], 0, keepdims=False)
    block_w = toeplitz_blocks(width, omega[0])
    block_h = block_w if height == width else toeplitz_blocks(height, omega[0])
    row_high, row_low = row_matrix(*block_w)
    col_high, col_low = column_matrix(*block_h)
    mat_w = whole((4, 2 * quart_w, 2 * quart_w))
    mat_h = whole((4, 2 * quart_h, 2 * quart_h))

    step = min(rows, 64)
    row_block = pl.BlockSpec((2, 1, step, width), lambda i: (0, 0, i, 0))
    quarter_block = pl.BlockSpec((4, 2, 2, step, quart_w), lambda i: (0, 0, 0, i, 0))
    quarter_shape = jax.ShapeDtypeStruct((4, 2, 2, rows, quart_w), jnp.float32)
    fields = pl.pallas_call(
        first_kernel,
        grid=(rows // step,),
        in_specs=[row_block, row_block, mat_w, mat_w],
        out_specs=quarter_block,
        out_shape=quarter_shape,
        compiler_params=params(),
    )(source_field, receiver_field, row_high, row_low)

    if row_count != 4:
        fields = fields.reshape(4, 2, 2, rows, row_count // 4, cols)
        fields = jnp.moveaxis(fields, 4, 1).reshape(row_count, 2, 2, rows, cols)
    fields = lax.all_to_all(fields, "row", split_axis=0, concat_axis=0, tiled=True)
    if row_count != 4:
        fields = fields.reshape(4, row_count // 4, 2, 2, rows, cols)
        fields = jnp.moveaxis(fields, 1, 3).reshape(4, 2, 2, quart_h, cols)
    slab_first = jnp.moveaxis(slab_first.reshape(rows, row_count, cols), 1, 0)
    slab_first = lax.all_to_all(slab_first, "row", split_axis=0, concat_axis=0, tiled=True)
    slab_first = slab_first.reshape(4, quart_h, cols)

    wide = min(cols, 128)
    col_block = pl.BlockSpec((4, 2, 2, quart_h, wide), lambda i: (0, 0, 0, 0, i))
    term_block = pl.BlockSpec((4, quart_h, wide), lambda i: (0, 0, i))
    fields, term = pl.pallas_call(
        middle_kernel,
        grid=(cols // wide,),
        in_specs=[scalar, col_block, term_block, mat_h, mat_h],
        out_specs=[col_block, term_block],
        out_shape=[
            jax.ShapeDtypeStruct((4, 2, 2, quart_h, cols), jnp.float32),
            jax.ShapeDtypeStruct((4, quart_h, cols), jnp.float32),
        ],
        compiler_params=params(),
    )(omega, fields, slab_first, col_high, col_low)

    if row_count != 4:
        fields = fields.reshape(4, 2, 2, row_count // 4, rows, cols)
        fields = jnp.moveaxis(fields, 3, 1).reshape(row_count, 2, 2, rows, cols)
    fields = lax.all_to_all(fields, "row", split_axis=0, concat_axis=0, tiled=True)
    if row_count != 4:
        fields = fields.reshape(4, row_count // 4, 2, 2, rows, cols)
        fields = jnp.moveaxis(fields, 1, 4).reshape(4, 2, 2, rows, quart_w)
    term = term.reshape(height, cols)
    if row_count == freq_count:
        part = lax.psum_scatter(term, "freq", scatter_dimension=0, tiled=True)
        pairs = [
            (r * freq_count + f, f * freq_count + r)
            for r in range(row_count)
            for f in range(freq_count)
        ]
        image_first = lax.ppermute(part, ("row", "freq"), pairs)
    else:
        term = lax.all_to_all(term, "row", split_axis=0, concat_axis=1, tiled=True)
        image_first = lax.psum_scatter(term, "freq", scatter_dimension=1, tiled=True)

    line_block = pl.BlockSpec((step, width), lambda i: (i, 0))
    field_shape = jax.ShapeDtypeStruct(source_field.shape, jnp.float32)
    source_out, receiver_out, term = pl.pallas_call(
        last_kernel,
        grid=(rows // step,),
        in_specs=[scalar, quarter_block, line_block, mat_w, mat_w],
        out_specs=[row_block, row_block, line_block],
        out_shape=[field_shape, field_shape, jax.ShapeDtypeStruct((rows, width), jnp.float32)],
        compiler_params=params(),
    )(omega, fields, slab_last, row_high, row_low)
    image_last = lax.psum_scatter(term, "freq", scatter_dimension=1, tiled=True)
    return source_out, receiver_out, jnp.stack([image_first, image_last])


def solution(mesh):
    in_specs = (
        P(None, ("shot", "freq"), "row", None),
        P(None, ("shot", "freq"), "row", None),
        P("freq", "row", None),
        P(),
        P(("shot", "freq")),
    )
    out_specs = (
        P(None, ("shot", "freq"), "row", None),
        P(None, ("shot", "freq"), "row", None),
        P("shot", "row", "freq"),
    )
    return jax.shard_map(body, mesh=mesh, in_specs=in_specs, out_specs=out_specs, check_vma=False)
```

```python
import math
from functools import partial

import jax
import jax.numpy as jnp
from jax import lax
from jax.experimental import pallas as pl
from jax.experimental.pallas import tpu as pltpu
from jax.sharding import PartitionSpec as P

dz_km = 0.01
dx_km = 0.0125
base_hertz = 3.0
step_hertz = 4.0
taper = 0.5
vmem_bytes = 56 * 1024 * 1024


def split_high_low(value):
    high = lax.reduce_precision(value, 8, 7)
    return high.astype(jnp.bfloat16), (value - high).astype(jnp.bfloat16)


def toeplitz_blocks(length, omega):
    quarter = length // 4
    place = jnp.arange(quarter, dtype=jnp.int32)
    kept = 4 * place[None, :] + jnp.arange(4, dtype=jnp.int32)[:, None]
    signed = jnp.where(kept * 2 < length, kept, kept - length)
    square = (signed.astype(jnp.float32) * (2.0 * math.pi / (length * dx_km))) ** 2
    kmax = math.pi / dx_km
    damp = jnp.exp(-taper * square / (kmax * kmax)) / float(length)
    phase = (-dz_km / omega) * square
    amp_r = (damp * jnp.cos(phase))[:, None, :]
    amp_i = (damp * jnp.sin(phase))[:, None, :]
    turns = (kept[:, None, :] * place[None, :, None] % length).astype(jnp.float32)
    turns = turns * (2.0 * math.pi / length)
    cos_v = jnp.cos(turns)
    sin_v = jnp.sin(turns)
    left = jnp.concatenate([cos_v * amp_r - sin_v * amp_i, sin_v * amp_r + cos_v * amp_i], axis=2)
    right = jnp.concatenate(
        [jnp.concatenate([cos_v, sin_v], axis=2), jnp.concatenate([-sin_v, cos_v], axis=2)], axis=1
    )
    both = jnp.einsum("kbm,kcm->kbc", left, right, precision=lax.Precision.HIGHEST)
    return both[:, :, :quarter], both[:, :, quarter:]


def pack(real, imag, sign):
    top = jnp.concatenate([real, -sign * imag], axis=2)
    low = jnp.concatenate([sign * imag, real], axis=2)
    return split_high_low(jnp.concatenate([top, low], axis=1))


def column_matrix(real, imag):
    return pack(real, imag, 1.0)


def row_matrix(real, imag):
    turned_r = jnp.stack([real[0], real[3], real[2], real[1]])
    turned_i = jnp.stack([imag[0], imag[3], imag[2], imag[1]])
    return pack(turned_r, turned_i, -1.0)


def butterfly(re, im, sign):
    sum_r, dif_r = re[0] + re[2], re[0] - re[2]
    sum_i, dif_i = im[0] + im[2], im[0] - im[2]
    odd_r, gap_r = re[1] + re[3], re[1] - re[3]
    odd_i, gap_i = im[1] + im[3], im[1] - im[3]
    if sign < 0:
        gap_r, gap_i = -gap_r, -gap_i
    out_r = [sum_r + odd_r, dif_r - gap_i, sum_r - odd_r, dif_r + gap_i]
    out_i = [sum_i + odd_i, dif_i + gap_r, sum_i - odd_i, dif_i - gap_r]
    return out_r, out_i


def halves(value):
    high = value.astype(jnp.bfloat16)
    return high, (value - high.astype(jnp.float32)).astype(jnp.bfloat16)


def dot(left, right):
    return jnp.dot(left, right, preferred_element_type=jnp.float32)


def filter_rows(re, im, high_ref, low_ref):
    quarter = re[0].shape[1]
    re, im = butterfly(re, im, -1)
    out_r, out_i = [], []
    for k in range(4):
        high, low = halves(jnp.concatenate([re[k], im[k]], axis=1))
        out = dot(high, high_ref[k]) + (dot(low, high_ref[k]) + dot(high, low_ref[k]))
        out_r.append(out[:, :quarter])
        out_i.append(out[:, quarter:])
    return butterfly(out_r, out_i, 1)


def filter_cols(re, im, high_ref, low_ref):
    quarter = re[0].shape[0]
    re, im = butterfly(re, im, -1)
    out_r, out_i = [], []
    for k in range(4):
        high, low = halves(jnp.concatenate([re[k], im[k]], axis=0))
        out = dot(high_ref[k], high) + (dot(high_ref[k], low) + dot(low_ref[k], high))
        out_r.append(out[:quarter])
        out_i.append(out[quarter:])
    return butterfly(out_r, out_i, 1)


def first_kernel(sign, field_ref, high_ref, low_ref, out_ref):
    quarter = field_ref.shape[3] // 4
    re, im = [], []
    for j in range(4):
        span = pl.ds(j * quarter, quarter)
        re.append(field_ref[0, 0, :, span])
        im.append(sign * field_ref[1, 0, :, span])
    re, im = filter_rows(re, im, high_ref, low_ref)
    for j in range(4):
        out_ref[j, 0] = re[j]
        out_ref[j, 1] = im[j]


def middle_step(cos_ref, sin_ref, field_ref, high_ref, low_ref, out_ref, keep):
    re = [field_ref[j, 0] for j in range(4)]
    im = [field_ref[j, 1] for j in range(4)]
    re, im = filter_cols(re, im, high_ref, low_ref)
    for j in range(4):
        cos_v, sin_v = cos_ref[j], sin_ref[j]
        re[j], im[j] = re[j] * cos_v - im[j] * sin_v, im[j] * cos_v + re[j] * sin_v
        keep(j, re[j], im[j])
    re, im = filter_cols(re, im, high_ref, low_ref)
    for j in range(4):
        out_ref[j, 0] = re[j]
        out_ref[j, 1] = im[j]


def middle_source(cos_ref, sin_ref, field_ref, high_ref, low_ref, out_ref, mid_ref):
    def keep(j, re, im):
        mid_ref[j, 0] = re
        mid_ref[j, 1] = im

    middle_step(cos_ref, sin_ref, field_ref, high_ref, low_ref, out_ref, keep)


def middle_receiver(cos_ref, sin_ref, field_ref, high_ref, low_ref, mid_ref, out_ref, term_ref):
    def keep(j, re, im):
        term_ref[j] = mid_ref[j, 0] * re - mid_ref[j, 1] * im

    middle_step(cos_ref, sin_ref, field_ref, high_ref, low_ref, out_ref, keep)


def last_step(cos_ref, sin_ref, field_ref, high_ref, low_ref, keep):
    quarter = field_ref.shape[3]
    re = [field_ref[j, 0] for j in range(4)]
    im = [field_ref[j, 1] for j in range(4)]
    re, im = filter_rows(re, im, high_ref, low_ref)
    for j in range(4):
        span = pl.ds(j * quarter, quarter)
        cos_v, sin_v = cos_ref[:, span], sin_ref[:, span]
        keep(span, re[j] * cos_v - im[j] * sin_v, im[j] * cos_v + re[j] * sin_v)


def last_source(cos_ref, sin_ref, field_ref, high_ref, low_ref, source_ref):
    def keep(span, re, im):
        source_ref[0, 0, :, span] = re
        source_ref[1, 0, :, span] = im

    last_step(cos_ref, sin_ref, field_ref, high_ref, low_ref, keep)


def last_receiver(cos_ref, sin_ref, field_ref, high_ref, low_ref, source_ref, receiver_ref, term_ref):
    def keep(span, re, im):
        term_ref[:, span] = source_ref[0, 0, :, span] * re - source_ref[1, 0, :, span] * im
        receiver_ref[0, 0, :, span] = re
        receiver_ref[1, 0, :, span] = -im

    last_step(cos_ref, sin_ref, field_ref, high_ref, low_ref, keep)


def params():
    return pltpu.CompilerParams(vmem_limit_bytes=vmem_bytes, dimension_semantics=("arbitrary",))


def whole(shape):
    return pl.BlockSpec(shape, lambda i: (0,) * len(shape))


def swap(blocks):
    return lax.all_to_all(blocks, "row", split_axis=0, concat_axis=0, tiled=True)


def body(source_field, receiver_field, slowness, owner, freq_index):
    rows, width = source_field.shape[2:]
    row_count = lax.axis_size("row")
    freq_count = lax.axis_size("freq")
    height = rows * row_count
    cols = width // row_count
    quart_w = width // 4
    quart_h = height // 4
    more = row_count // 4
    omega = 2.0 * math.pi * (base_hertz + step_hertz * freq_index.astype(jnp.float32))

    def turning(slab):
        theta = slab * (omega[0] * dz_km)
        return jnp.cos(theta), jnp.sin(theta)

    def owned(depth):
        return jnp.where(lax.axis_index("freq") == owner[depth], slowness[0], 0.0)

    turned = swap(jnp.moveaxis(owned(0).reshape(rows, row_count, cols), 1, 0))
    source_field, turned = lax.optimization_barrier((source_field, turned))
    piece = lax.psum_scatter(turned, "freq", scatter_dimension=0, tiled=True)
    receiver_field, piece = lax.optimization_barrier((receiver_field, piece))
    slab_first = lax.all_gather(piece, "freq", axis=0, tiled=True)
    slab, slab_first = lax.optimization_barrier((owned(1), slab_first))
    slab_last = lax.psum(slab, "freq")
    turn_first = turning(slab_first.reshape(4, quart_h, cols))
    turn_last = turning(slab_last)

    block_w = toeplitz_blocks(width, omega[0])
    block_h = block_w if height == width else toeplitz_blocks(height, omega[0])
    row_high, row_low = row_matrix(*block_w)
    col_high, col_low = column_matrix(*block_h)
    mat_w = whole((4, 2 * quart_w, 2 * quart_w))
    mat_h = whole((4, 2 * quart_h, 2 * quart_h))

    step = min(rows, 128)
    row_block = pl.BlockSpec((2, 1, step, width), lambda i: (0, 0, i, 0))
    quarter_block = pl.BlockSpec((4, 2, step, quart_w), lambda i: (0, 0, i, 0))
    line_block = pl.BlockSpec((step, width), lambda i: (i, 0))
    col_block = pl.BlockSpec((4, 2, quart_h, cols), lambda i: (0, 0, 0, 0))
    term_block = pl.BlockSpec((4, quart_h, cols), lambda i: (0, 0, 0))
    quarter_shape = jax.ShapeDtypeStruct((4, 2, rows, quart_w), jnp.float32)
    col_shape = jax.ShapeDtypeStruct((4, 2, quart_h, cols), jnp.float32)
    term_shape = jax.ShapeDtypeStruct((4, quart_h, cols), jnp.float32)
    line_shape = jax.ShapeDtypeStruct((rows, width), jnp.float32)
    field_shape = jax.ShapeDtypeStruct(source_field.shape, jnp.float32)

    def first(field, sign):
        return pl.pallas_call(
            partial(first_kernel, sign),
            grid=(rows // step,),
            in_specs=[row_block, mat_w, mat_w],
            out_specs=quarter_block,
            out_shape=quarter_shape,
            compiler_params=params(),
        )(field, row_high, row_low)

    def to_cols(fields):
        if more > 1:
            fields = fields.reshape(4, 2, rows, more, cols)
            fields = jnp.moveaxis(fields, 3, 1).reshape(row_count, 2, rows, cols)
        fields = swap(fields)
        if more > 1:
            fields = fields.reshape(4, more, 2, rows, cols)
            fields = jnp.moveaxis(fields, 1, 2).reshape(4, 2, quart_h, cols)
        return fields

    def to_rows(fields):
        if more > 1:
            fields = fields.reshape(4, 2, more, rows, cols)
            fields = jnp.moveaxis(fields, 2, 1).reshape(row_count, 2, rows, cols)
        fields = swap(fields)
        if more > 1:
            fields = fields.reshape(4, more, 2, rows, cols)
            fields = jnp.moveaxis(fields, 1, 3).reshape(4, 2, rows, quart_w)
        return fields

    source = to_cols(first(source_field, 1.0))
    receiver = to_cols(first(receiver_field, -1.0))
    source, middle = pl.pallas_call(
        middle_source,
        grid=(1,),
        in_specs=[term_block, term_block, col_block, mat_h, mat_h],
        out_specs=[col_block, col_block],
        out_shape=[col_shape, col_shape],
        compiler_params=params(),
    )(*turn_first, source, col_high, col_low)
    source = to_rows(source)
    receiver, term = pl.pallas_call(
        middle_receiver,
        grid=(1,),
        in_specs=[term_block, term_block, col_block, mat_h, mat_h, col_block],
        out_specs=[col_block, term_block],
        out_shape=[col_shape, term_shape],
        compiler_params=params(),
    )(*turn_first, receiver, col_high, col_low, middle)
    receiver = to_rows(receiver)

    term = term.reshape(height, cols)
    if row_count == freq_count:
        part = lax.psum_scatter(term, "freq", scatter_dimension=0, tiled=True)
        pairs = [
            (r * freq_count + f, f * freq_count + r)
            for r in range(row_count)
            for f in range(freq_count)
        ]
        image_first = lax.ppermute(part, ("row", "freq"), pairs)
    else:
        term = lax.all_to_all(term, "row", split_axis=0, concat_axis=1, tiled=True)
        image_first = lax.psum_scatter(term, "freq", scatter_dimension=1, tiled=True)

    source_out = pl.pallas_call(
        last_source,
        grid=(rows // step,),
        in_specs=[line_block, line_block, quarter_block, mat_w, mat_w],
        out_specs=row_block,
        out_shape=field_shape,
        compiler_params=params(),
    )(*turn_last, source, row_high, row_low)
    receiver_out, term = pl.pallas_call(
        last_receiver,
        grid=(rows // step,),
        in_specs=[line_block, line_block, quarter_block, mat_w, mat_w, row_block],
        out_specs=[row_block, line_block],
        out_shape=[field_shape, line_shape],
        compiler_params=params(),
    )(*turn_last, receiver, row_high, row_low, source_out)
    image_last = lax.psum_scatter(term, "freq", scatter_dimension=1, tiled=True)
    return source_out, receiver_out, jnp.stack([image_first, image_last])


def solution(mesh):
    in_specs = (
        P(None, ("shot", "freq"), "row", None),
        P(None, ("shot", "freq"), "row", None),
        P("freq", "row", None),
        P(),
        P(("shot", "freq")),
    )
    out_specs = (
        P(None, ("shot", "freq"), "row", None),
        P(None, ("shot", "freq"), "row", None),
        P("shot", "row", "freq"),
    )
    return jax.shard_map(body, mesh=mesh, in_specs=in_specs, out_specs=out_specs, check_vma=False)
```

```python
import math
from functools import partial

import jax
import jax.numpy as jnp
from jax import lax
from jax.experimental import pallas as pl
from jax.experimental.pallas import tpu as pltpu
from jax.sharding import PartitionSpec as P

dz_km = 0.01
dx_km = 0.0125
base_hertz = 3.0
step_hertz = 4.0
taper = 0.5
vmem_bytes = 56 * 1024 * 1024


def split_high_low(value):
    high = lax.reduce_precision(value, 8, 7)
    return high.astype(jnp.bfloat16), (value - high).astype(jnp.bfloat16)


def toeplitz_blocks(length, omega):
    quarter = length // 4
    place = jnp.arange(quarter, dtype=jnp.int32)
    kept = 4 * place[None, :] + jnp.arange(4, dtype=jnp.int32)[:, None]
    signed = jnp.where(kept * 2 < length, kept, kept - length)
    square = (signed.astype(jnp.float32) * (2.0 * math.pi / (length * dx_km))) ** 2
    kmax = math.pi / dx_km
    damp = jnp.exp(-taper * square / (kmax * kmax)) / float(length)
    phase = (-dz_km / omega) * square
    amp_r = (damp * jnp.cos(phase))[:, None, :]
    amp_i = (damp * jnp.sin(phase))[:, None, :]
    turns = (kept[:, None, :] * place[None, :, None] % length).astype(jnp.float32)
    turns = turns * (2.0 * math.pi / length)
    cos_v = jnp.cos(turns)
    sin_v = jnp.sin(turns)
    left = jnp.concatenate([cos_v * amp_r - sin_v * amp_i, sin_v * amp_r + cos_v * amp_i], axis=2)
    right = jnp.concatenate(
        [jnp.concatenate([cos_v, sin_v], axis=2), jnp.concatenate([-sin_v, cos_v], axis=2)], axis=1
    )
    both = jnp.einsum("kbm,kcm->kbc", left, right, precision=lax.Precision.HIGHEST)
    return both[:, :, :quarter], both[:, :, quarter:]


def pack(real, imag, sign):
    top = jnp.concatenate([real, -sign * imag], axis=2)
    low = jnp.concatenate([sign * imag, real], axis=2)
    return split_high_low(jnp.concatenate([top, low], axis=1))


def column_matrix(real, imag):
    return pack(real, imag, 1.0)


def row_matrix(real, imag):
    turned_r = jnp.stack([real[0], real[3], real[2], real[1]])
    turned_i = jnp.stack([imag[0], imag[3], imag[2], imag[1]])
    return pack(turned_r, turned_i, -1.0)


def butterfly(re, im, sign):
    sum_r, dif_r = re[0] + re[2], re[0] - re[2]
    sum_i, dif_i = im[0] + im[2], im[0] - im[2]
    odd_r, gap_r = re[1] + re[3], re[1] - re[3]
    odd_i, gap_i = im[1] + im[3], im[1] - im[3]
    if sign < 0:
        gap_r, gap_i = -gap_r, -gap_i
    out_r = [sum_r + odd_r, dif_r - gap_i, sum_r - odd_r, dif_r + gap_i]
    out_i = [sum_i + odd_i, dif_i + gap_r, sum_i - odd_i, dif_i - gap_r]
    return out_r, out_i


def halves(value):
    high = value.astype(jnp.bfloat16)
    return high, (value - high.astype(jnp.float32)).astype(jnp.bfloat16)


def dot(left, right):
    return jnp.dot(left, right, preferred_element_type=jnp.float32)


def filter_rows(re, im, high_ref, low_ref):
    quarter = re[0].shape[1]
    re, im = butterfly(re, im, -1)
    out_r, out_i = [], []
    for k in range(4):
        high, low = halves(jnp.concatenate([re[k], im[k]], axis=1))
        out = dot(high, high_ref[k]) + (dot(low, high_ref[k]) + dot(high, low_ref[k]))
        out_r.append(out[:, :quarter])
        out_i.append(out[:, quarter:])
    return butterfly(out_r, out_i, 1)


def filter_cols(re, im, high_ref, low_ref):
    quarter = re[0].shape[0]
    re, im = butterfly(re, im, -1)
    out_r, out_i = [], []
    for k in range(4):
        high, low = halves(jnp.concatenate([re[k], im[k]], axis=0))
        out = dot(high_ref[k], high) + (dot(high_ref[k], low) + dot(low_ref[k], high))
        out_r.append(out[:quarter])
        out_i.append(out[quarter:])
    return butterfly(out_r, out_i, 1)


def first_kernel(sign, field_ref, high_ref, low_ref, out_ref):
    quarter = field_ref.shape[3] // 4
    re, im = [], []
    for j in range(4):
        span = pl.ds(j * quarter, quarter)
        re.append(field_ref[0, 0, :, span])
        im.append(sign * field_ref[1, 0, :, span])
    re, im = filter_rows(re, im, high_ref, low_ref)
    for j in range(4):
        out_ref[j, 0] = re[j]
        out_ref[j, 1] = im[j]


def middle_step(cos_ref, sin_ref, field_ref, high_ref, low_ref, out_ref, keep):
    re = [field_ref[j, 0] for j in range(4)]
    im = [field_ref[j, 1] for j in range(4)]
    re, im = filter_cols(re, im, high_ref, low_ref)
    for j in range(4):
        cos_v, sin_v = cos_ref[j], sin_ref[j]
        re[j], im[j] = re[j] * cos_v - im[j] * sin_v, im[j] * cos_v + re[j] * sin_v
        keep(j, re[j], im[j])
    re, im = filter_cols(re, im, high_ref, low_ref)
    for j in range(4):
        out_ref[j, 0] = re[j]
        out_ref[j, 1] = im[j]


def middle_source(cos_ref, sin_ref, field_ref, high_ref, low_ref, out_ref, mid_ref):
    def keep(j, re, im):
        mid_ref[j, 0] = re
        mid_ref[j, 1] = im

    middle_step(cos_ref, sin_ref, field_ref, high_ref, low_ref, out_ref, keep)


def middle_receiver(cos_ref, sin_ref, field_ref, high_ref, low_ref, mid_ref, out_ref, term_ref):
    def keep(j, re, im):
        term_ref[j] = mid_ref[j, 0] * re - mid_ref[j, 1] * im

    middle_step(cos_ref, sin_ref, field_ref, high_ref, low_ref, out_ref, keep)


def last_step(cos_ref, sin_ref, field_ref, high_ref, low_ref, keep):
    quarter = field_ref.shape[3]
    re = [field_ref[j, 0] for j in range(4)]
    im = [field_ref[j, 1] for j in range(4)]
    re, im = filter_rows(re, im, high_ref, low_ref)
    for j in range(4):
        span = pl.ds(j * quarter, quarter)
        cos_v, sin_v = cos_ref[:, span], sin_ref[:, span]
        keep(span, re[j] * cos_v - im[j] * sin_v, im[j] * cos_v + re[j] * sin_v)


def last_source(cos_ref, sin_ref, field_ref, high_ref, low_ref, source_ref):
    def keep(span, re, im):
        source_ref[0, 0, :, span] = re
        source_ref[1, 0, :, span] = im

    last_step(cos_ref, sin_ref, field_ref, high_ref, low_ref, keep)


def last_receiver(cos_ref, sin_ref, field_ref, high_ref, low_ref, source_ref, receiver_ref, term_ref):
    def keep(span, re, im):
        term_ref[:, span] = source_ref[0, 0, :, span] * re - source_ref[1, 0, :, span] * im
        receiver_ref[0, 0, :, span] = re
        receiver_ref[1, 0, :, span] = -im

    last_step(cos_ref, sin_ref, field_ref, high_ref, low_ref, keep)


def params():
    return pltpu.CompilerParams(vmem_limit_bytes=vmem_bytes, dimension_semantics=("arbitrary",))


def whole(shape):
    return pl.BlockSpec(shape, lambda i: (0,) * len(shape))


def swap(blocks):
    return lax.all_to_all(blocks, "row", split_axis=0, concat_axis=0, tiled=True)


def body(source_field, receiver_field, slowness, owner, freq_index):
    rows, width = source_field.shape[2:]
    row_count = lax.axis_size("row")
    freq_count = lax.axis_size("freq")
    height = rows * row_count
    cols = width // row_count
    quart_w = width // 4
    quart_h = height // 4
    more = row_count // 4
    omega = 2.0 * math.pi * (base_hertz + step_hertz * freq_index.astype(jnp.float32))

    def turning(slab):
        theta = slab * (omega[0] * dz_km)
        return jnp.cos(theta), jnp.sin(theta)

    def owned(depth):
        return jnp.where(lax.axis_index("freq") == owner[depth], slowness[0], 0.0)

    turned = swap(jnp.moveaxis(owned(0).reshape(rows, row_count, cols), 1, 0))
    piece_last = lax.psum_scatter(owned(1), "freq", scatter_dimension=0, tiled=True)
    source_field, turned = lax.optimization_barrier((source_field, turned))
    turned, piece_last = lax.optimization_barrier((turned, piece_last))
    piece = lax.psum_scatter(turned, "freq", scatter_dimension=0, tiled=True)
    receiver_field, piece = lax.optimization_barrier((receiver_field, piece))
    slab_first = lax.all_gather(piece, "freq", axis=0, tiled=True)
    piece_last, slab_first = lax.optimization_barrier((piece_last, slab_first))
    slab_last = lax.all_gather(piece_last, "freq", axis=0, tiled=True)
    turn_first = turning(slab_first.reshape(4, quart_h, cols))

    block_w = toeplitz_blocks(width, omega[0])
    block_h = block_w if height == width else toeplitz_blocks(height, omega[0])
    row_high, row_low = row_matrix(*block_w)
    col_high, col_low = column_matrix(*block_h)
    mat_w = whole((4, 2 * quart_w, 2 * quart_w))
    mat_h = whole((4, 2 * quart_h, 2 * quart_h))

    step = min(rows, 128)
    row_block = pl.BlockSpec((2, 1, step, width), lambda i: (0, 0, i, 0))
    quarter_block = pl.BlockSpec((4, 2, step, quart_w), lambda i: (0, 0, i, 0))
    line_block = pl.BlockSpec((step, width), lambda i: (i, 0))
    col_block = pl.BlockSpec((4, 2, quart_h, cols), lambda i: (0, 0, 0, 0))
    term_block = pl.BlockSpec((4, quart_h, cols), lambda i: (0, 0, 0))
    quarter_shape = jax.ShapeDtypeStruct((4, 2, rows, quart_w), jnp.float32)
    col_shape = jax.ShapeDtypeStruct((4, 2, quart_h, cols), jnp.float32)
    term_shape = jax.ShapeDtypeStruct((4, quart_h, cols), jnp.float32)
    line_shape = jax.ShapeDtypeStruct((rows, width), jnp.float32)
    field_shape = jax.ShapeDtypeStruct(source_field.shape, jnp.float32)

    def first(field, sign):
        return pl.pallas_call(
            partial(first_kernel, sign),
            grid=(rows // step,),
            in_specs=[row_block, mat_w, mat_w],
            out_specs=quarter_block,
            out_shape=quarter_shape,
            compiler_params=params(),
        )(field, row_high, row_low)

    def to_cols(fields):
        if more > 1:
            fields = fields.reshape(4, 2, rows, more, cols)
            fields = jnp.moveaxis(fields, 3, 1).reshape(row_count, 2, rows, cols)
        fields = swap(fields)
        if more > 1:
            fields = fields.reshape(4, more, 2, rows, cols)
            fields = jnp.moveaxis(fields, 1, 2).reshape(4, 2, quart_h, cols)
        return fields

    def to_rows(fields):
        if more > 1:
            fields = fields.reshape(4, 2, more, rows, cols)
            fields = jnp.moveaxis(fields, 2, 1).reshape(row_count, 2, rows, cols)
        fields = swap(fields)
        if more > 1:
            fields = fields.reshape(4, more, 2, rows, cols)
            fields = jnp.moveaxis(fields, 1, 3).reshape(4, 2, rows, quart_w)
        return fields

    source = to_cols(first(source_field, 1.0))
    receiver = to_cols(first(receiver_field, -1.0))
    source, middle = pl.pallas_call(
        middle_source,
        grid=(1,),
        in_specs=[term_block, term_block, col_block, mat_h, mat_h],
        out_specs=[col_block, col_block],
        out_shape=[col_shape, col_shape],
        compiler_params=params(),
    )(*turn_first, source, col_high, col_low)
    source = to_rows(source)
    receiver, term = pl.pallas_call(
        middle_receiver,
        grid=(1,),
        in_specs=[term_block, term_block, col_block, mat_h, mat_h, col_block],
        out_specs=[col_block, term_block],
        out_shape=[col_shape, term_shape],
        compiler_params=params(),
    )(*turn_first, receiver, col_high, col_low, middle)
    receiver, term, slab_last = lax.optimization_barrier((receiver, term, slab_last))
    turn_last = turning(slab_last)
    receiver = to_rows(receiver)

    term = term.reshape(height, cols)
    if row_count == freq_count:
        part = lax.psum_scatter(term, "freq", scatter_dimension=0, tiled=True)
        pairs = [
            (r * freq_count + f, f * freq_count + r)
            for r in range(row_count)
            for f in range(freq_count)
        ]
        image_first = lax.ppermute(part, ("row", "freq"), pairs)
    else:
        term = lax.all_to_all(term, "row", split_axis=0, concat_axis=1, tiled=True)
        image_first = lax.psum_scatter(term, "freq", scatter_dimension=1, tiled=True)

    source_out = pl.pallas_call(
        last_source,
        grid=(rows // step,),
        in_specs=[line_block, line_block, quarter_block, mat_w, mat_w],
        out_specs=row_block,
        out_shape=field_shape,
        compiler_params=params(),
    )(*turn_last, source, row_high, row_low)
    receiver_out, term = pl.pallas_call(
        last_receiver,
        grid=(rows // step,),
        in_specs=[line_block, line_block, quarter_block, mat_w, mat_w, row_block],
        out_specs=[row_block, line_block],
        out_shape=[field_shape, line_shape],
        compiler_params=params(),
    )(*turn_last, receiver, row_high, row_low, source_out)
    image_last = lax.psum_scatter(term, "freq", scatter_dimension=1, tiled=True)
    return source_out, receiver_out, jnp.stack([image_first, image_last])


def solution(mesh):
    in_specs = (
        P(None, ("shot", "freq"), "row", None),
        P(None, ("shot", "freq"), "row", None),
        P("freq", "row", None),
        P(),
        P(("shot", "freq")),
    )
    out_specs = (
        P(None, ("shot", "freq"), "row", None),
        P(None, ("shot", "freq"), "row", None),
        P("shot", "row", "freq"),
    )
    return jax.shard_map(body, mesh=mesh, in_specs=in_specs, out_specs=out_specs, check_vma=False)
```

```python
import math
from functools import partial

import jax
import jax.numpy as jnp
from jax import lax
from jax.experimental import pallas as pl
from jax.experimental.pallas import tpu as pltpu
from jax.sharding import PartitionSpec as P

dz_km = 0.01
dx_km = 0.0125
base_hertz = 3.0
step_hertz = 4.0
taper = 0.5
vmem_bytes = 56 * 1024 * 1024


def split_high_low(value):
    high = lax.reduce_precision(value, 8, 7)
    return high.astype(jnp.bfloat16), (value - high).astype(jnp.bfloat16)


def toeplitz_blocks(length, omega):
    quarter = length // 4
    place = jnp.arange(quarter, dtype=jnp.int32)
    kept = 4 * place[None, :] + jnp.arange(4, dtype=jnp.int32)[:, None]
    signed = jnp.where(kept * 2 < length, kept, kept - length)
    square = (signed.astype(jnp.float32) * (2.0 * math.pi / (length * dx_km))) ** 2
    kmax = math.pi / dx_km
    damp = jnp.exp(-taper * square / (kmax * kmax)) / float(length)
    phase = (-dz_km / omega) * square
    amp_r = (damp * jnp.cos(phase))[:, None, :]
    amp_i = (damp * jnp.sin(phase))[:, None, :]
    turns = (kept[:, None, :] * place[None, :, None] % length).astype(jnp.float32)
    turns = turns * (2.0 * math.pi / length)
    cos_v = jnp.cos(turns)
    sin_v = jnp.sin(turns)
    left = jnp.concatenate([cos_v * amp_r - sin_v * amp_i, sin_v * amp_r + cos_v * amp_i], axis=2)
    right = jnp.concatenate(
        [jnp.concatenate([cos_v, sin_v], axis=2), jnp.concatenate([-sin_v, cos_v], axis=2)], axis=1
    )
    both = jnp.einsum("kbm,kcm->kbc", left, right, precision=lax.Precision.HIGHEST)
    return both[:, :, :quarter], both[:, :, quarter:]


def pack(real, imag, sign):
    top = jnp.concatenate([real, -sign * imag], axis=2)
    low = jnp.concatenate([sign * imag, real], axis=2)
    return split_high_low(jnp.concatenate([top, low], axis=1))


def column_matrix(real, imag):
    return pack(real, imag, 1.0)


def row_matrix(real, imag):
    turned_r = jnp.stack([real[0], real[3], real[2], real[1]])
    turned_i = jnp.stack([imag[0], imag[3], imag[2], imag[1]])
    return pack(turned_r, turned_i, -1.0)


def butterfly(re, im, sign):
    sum_r, dif_r = re[0] + re[2], re[0] - re[2]
    sum_i, dif_i = im[0] + im[2], im[0] - im[2]
    odd_r, gap_r = re[1] + re[3], re[1] - re[3]
    odd_i, gap_i = im[1] + im[3], im[1] - im[3]
    if sign < 0:
        gap_r, gap_i = -gap_r, -gap_i
    out_r = [sum_r + odd_r, dif_r - gap_i, sum_r - odd_r, dif_r + gap_i]
    out_i = [sum_i + odd_i, dif_i + gap_r, sum_i - odd_i, dif_i - gap_r]
    return out_r, out_i


def halves(value):
    high = value.astype(jnp.bfloat16)
    return high, (value - high.astype(jnp.float32)).astype(jnp.bfloat16)


def dot(left, right):
    return jnp.dot(left, right, preferred_element_type=jnp.float32)


def filter_rows(re, im, high_ref, low_ref):
    quarter = re[0].shape[1]
    re, im = butterfly(re, im, -1)
    out_r, out_i = [], []
    for k in range(4):
        high, low = halves(jnp.concatenate([re[k], im[k]], axis=1))
        out = dot(high, high_ref[k]) + (dot(low, high_ref[k]) + dot(high, low_ref[k]))
        out_r.append(out[:, :quarter])
        out_i.append(out[:, quarter:])
    return butterfly(out_r, out_i, 1)


def filter_cols(re, im, high_ref, low_ref):
    quarter = re[0].shape[0]
    re, im = butterfly(re, im, -1)
    out_r, out_i = [], []
    for k in range(4):
        high, low = halves(jnp.concatenate([re[k], im[k]], axis=0))
        out = dot(high_ref[k], high) + (dot(high_ref[k], low) + dot(low_ref[k], high))
        out_r.append(out[:quarter])
        out_i.append(out[quarter:])
    return butterfly(out_r, out_i, 1)


def first_kernel(sign, field_ref, high_ref, low_ref, out_ref):
    quarter = field_ref.shape[3] // 4
    re, im = [], []
    for j in range(4):
        span = pl.ds(j * quarter, quarter)
        re.append(field_ref[0, 0, :, span])
        im.append(sign * field_ref[1, 0, :, span])
    re, im = filter_rows(re, im, high_ref, low_ref)
    for j in range(4):
        out_ref[j, 0] = re[j]
        out_ref[j, 1] = im[j]


def middle_step(cos_ref, sin_ref, field_ref, high_ref, low_ref, out_ref, keep):
    re = [field_ref[j, 0] for j in range(4)]
    im = [field_ref[j, 1] for j in range(4)]
    re, im = filter_cols(re, im, high_ref, low_ref)
    for j in range(4):
        cos_v, sin_v = cos_ref[j], sin_ref[j]
        re[j], im[j] = re[j] * cos_v - im[j] * sin_v, im[j] * cos_v + re[j] * sin_v
        keep(j, re[j], im[j])
    re, im = filter_cols(re, im, high_ref, low_ref)
    for j in range(4):
        out_ref[j, 0] = re[j]
        out_ref[j, 1] = im[j]


def middle_source(cos_ref, sin_ref, field_ref, high_ref, low_ref, out_ref, mid_ref):
    def keep(j, re, im):
        mid_ref[j, 0] = re
        mid_ref[j, 1] = im

    middle_step(cos_ref, sin_ref, field_ref, high_ref, low_ref, out_ref, keep)


def middle_receiver(cos_ref, sin_ref, field_ref, high_ref, low_ref, mid_ref, out_ref, term_ref):
    def keep(j, re, im):
        term_ref[j] = mid_ref[j, 0] * re - mid_ref[j, 1] * im

    middle_step(cos_ref, sin_ref, field_ref, high_ref, low_ref, out_ref, keep)


def last_step(cos_ref, sin_ref, field_ref, high_ref, low_ref, keep):
    quarter = field_ref.shape[3]
    re = [field_ref[j, 0] for j in range(4)]
    im = [field_ref[j, 1] for j in range(4)]
    re, im = filter_rows(re, im, high_ref, low_ref)
    for j in range(4):
        span = pl.ds(j * quarter, quarter)
        cos_v, sin_v = cos_ref[:, span], sin_ref[:, span]
        keep(span, re[j] * cos_v - im[j] * sin_v, im[j] * cos_v + re[j] * sin_v)


def last_source(cos_ref, sin_ref, field_ref, high_ref, low_ref, source_ref):
    def keep(span, re, im):
        source_ref[0, 0, :, span] = re
        source_ref[1, 0, :, span] = im

    last_step(cos_ref, sin_ref, field_ref, high_ref, low_ref, keep)


def last_receiver(cos_ref, sin_ref, field_ref, high_ref, low_ref, source_ref, receiver_ref, term_ref):
    def keep(span, re, im):
        term_ref[span.start // span.size] = (
            source_ref[0, 0, :, span] * re - source_ref[1, 0, :, span] * im
        )
        receiver_ref[0, 0, :, span] = re
        receiver_ref[1, 0, :, span] = -im

    last_step(cos_ref, sin_ref, field_ref, high_ref, low_ref, keep)


def params():
    return pltpu.CompilerParams(vmem_limit_bytes=vmem_bytes, dimension_semantics=("arbitrary",))


def whole(shape):
    return pl.BlockSpec(shape, lambda i: (0,) * len(shape))


def swap(blocks):
    return lax.all_to_all(blocks, "row", split_axis=0, concat_axis=0, tiled=True)


def sum_strips(strips):
    count = strips.shape[0]
    me = lax.axis_index("freq")
    total = lax.dynamic_index_in_dim(strips, me, 0, keepdims=False)
    for shift in range(1, count):
        sent = lax.dynamic_index_in_dim(strips, (me + shift) % count, 0, keepdims=False)
        total = total + lax.ppermute(sent, "freq", [(i, (i + shift) % count) for i in range(count)])
    return total


def body(source_field, receiver_field, slowness, owner, freq_index):
    rows, width = source_field.shape[2:]
    row_count = lax.axis_size("row")
    freq_count = lax.axis_size("freq")
    height = rows * row_count
    cols = width // row_count
    quart_w = width // 4
    quart_h = height // 4
    more = row_count // 4
    omega = 2.0 * math.pi * (base_hertz + step_hertz * freq_index.astype(jnp.float32))

    def turning(slab):
        theta = slab * (omega[0] * dz_km)
        return jnp.cos(theta), jnp.sin(theta)

    def owned(depth):
        return jnp.where(lax.axis_index("freq") == owner[depth], slowness[0], 0.0)

    turned = swap(jnp.moveaxis(owned(0).reshape(rows, row_count, cols), 1, 0))
    piece_last = lax.psum_scatter(owned(1), "freq", scatter_dimension=0, tiled=True)
    source_field, turned = lax.optimization_barrier((source_field, turned))
    turned, piece_last = lax.optimization_barrier((turned, piece_last))
    piece = lax.psum_scatter(turned, "freq", scatter_dimension=0, tiled=True)
    receiver_field, piece = lax.optimization_barrier((receiver_field, piece))
    slab_first = lax.all_gather(piece, "freq", axis=0, tiled=True)
    piece_last, slab_first = lax.optimization_barrier((piece_last, slab_first))
    slab_last = lax.all_gather(piece_last, "freq", axis=0, tiled=True)
    turn_first = turning(slab_first.reshape(4, quart_h, cols))

    block_w = toeplitz_blocks(width, omega[0])
    block_h = block_w if height == width else toeplitz_blocks(height, omega[0])
    row_high, row_low = row_matrix(*block_w)
    col_high, col_low = column_matrix(*block_h)
    mat_w = whole((4, 2 * quart_w, 2 * quart_w))
    mat_h = whole((4, 2 * quart_h, 2 * quart_h))

    step = min(rows, 128)
    row_block = pl.BlockSpec((2, 1, step, width), lambda i: (0, 0, i, 0))
    quarter_block = pl.BlockSpec((4, 2, step, quart_w), lambda i: (0, 0, i, 0))
    line_block = pl.BlockSpec((step, width), lambda i: (i, 0))
    col_block = pl.BlockSpec((4, 2, quart_h, cols), lambda i: (0, 0, 0, 0))
    term_block = pl.BlockSpec((4, quart_h, cols), lambda i: (0, 0, 0))
    quarter_shape = jax.ShapeDtypeStruct((4, 2, rows, quart_w), jnp.float32)
    col_shape = jax.ShapeDtypeStruct((4, 2, quart_h, cols), jnp.float32)
    term_shape = jax.ShapeDtypeStruct((4, quart_h, cols), jnp.float32)
    strip_block = pl.BlockSpec((4, step, quart_w), lambda i: (0, i, 0))
    strip_shape = jax.ShapeDtypeStruct((4, rows, quart_w), jnp.float32)
    field_shape = jax.ShapeDtypeStruct(source_field.shape, jnp.float32)

    def first(field, sign):
        return pl.pallas_call(
            partial(first_kernel, sign),
            grid=(rows // step,),
            in_specs=[row_block, mat_w, mat_w],
            out_specs=quarter_block,
            out_shape=quarter_shape,
            compiler_params=params(),
        )(field, row_high, row_low)

    def to_cols(fields):
        if more > 1:
            fields = fields.reshape(4, 2, rows, more, cols)
            fields = jnp.moveaxis(fields, 3, 1).reshape(row_count, 2, rows, cols)
        fields = swap(fields)
        if more > 1:
            fields = fields.reshape(4, more, 2, rows, cols)
            fields = jnp.moveaxis(fields, 1, 2).reshape(4, 2, quart_h, cols)
        return fields

    def to_rows(fields):
        if more > 1:
            fields = fields.reshape(4, 2, more, rows, cols)
            fields = jnp.moveaxis(fields, 2, 1).reshape(row_count, 2, rows, cols)
        fields = swap(fields)
        if more > 1:
            fields = fields.reshape(4, more, 2, rows, cols)
            fields = jnp.moveaxis(fields, 1, 3).reshape(4, 2, rows, quart_w)
        return fields

    source = to_cols(first(source_field, 1.0))
    receiver = to_cols(first(receiver_field, -1.0))
    source, middle = pl.pallas_call(
        middle_source,
        grid=(1,),
        in_specs=[term_block, term_block, col_block, mat_h, mat_h],
        out_specs=[col_block, col_block],
        out_shape=[col_shape, col_shape],
        compiler_params=params(),
    )(*turn_first, source, col_high, col_low)
    source = to_rows(source)
    receiver, term = pl.pallas_call(
        middle_receiver,
        grid=(1,),
        in_specs=[term_block, term_block, col_block, mat_h, mat_h, col_block],
        out_specs=[col_block, term_block],
        out_shape=[col_shape, term_shape],
        compiler_params=params(),
    )(*turn_first, receiver, col_high, col_low, middle)
    receiver, term, slab_last = lax.optimization_barrier((receiver, term, slab_last))
    turn_last = turning(slab_last)
    receiver = to_rows(receiver)

    term = term.reshape(height, cols)
    if row_count == freq_count:
        part = lax.psum_scatter(term, "freq", scatter_dimension=0, tiled=True)
        pairs = [
            (r * freq_count + f, f * freq_count + r)
            for r in range(row_count)
            for f in range(freq_count)
        ]
        image_first = lax.ppermute(part, ("row", "freq"), pairs)
    else:
        term = lax.all_to_all(term, "row", split_axis=0, concat_axis=1, tiled=True)
        image_first = lax.psum_scatter(term, "freq", scatter_dimension=1, tiled=True)

    source_out = pl.pallas_call(
        last_source,
        grid=(rows // step,),
        in_specs=[line_block, line_block, quarter_block, mat_w, mat_w],
        out_specs=row_block,
        out_shape=field_shape,
        compiler_params=params(),
    )(*turn_last, source, row_high, row_low)
    receiver_out, term = pl.pallas_call(
        last_receiver,
        grid=(rows // step,),
        in_specs=[line_block, line_block, quarter_block, mat_w, mat_w, row_block],
        out_specs=[row_block, strip_block],
        out_shape=[field_shape, strip_shape],
        compiler_params=params(),
    )(*turn_last, receiver, row_high, row_low, source_out)
    if freq_count == 4:
        image_last = sum_strips(term)
    else:
        term = jnp.moveaxis(term, 0, 1).reshape(rows, width)
        image_last = lax.psum_scatter(term, "freq", scatter_dimension=1, tiled=True)
    return source_out, receiver_out, jnp.stack([image_first, image_last])


def solution(mesh):
    in_specs = (
        P(None, ("shot", "freq"), "row", None),
        P(None, ("shot", "freq"), "row", None),
        P("freq", "row", None),
        P(),
        P(("shot", "freq")),
    )
    out_specs = (
        P(None, ("shot", "freq"), "row", None),
        P(None, ("shot", "freq"), "row", None),
        P("shot", "row", "freq"),
    )
    return jax.shard_map(body, mesh=mesh, in_specs=in_specs, out_specs=out_specs, check_vma=False)
```

```python
import math
from functools import partial

import jax
import jax.numpy as jnp
from jax import lax
from jax.experimental import pallas as pl
from jax.experimental.pallas import tpu as pltpu
from jax.sharding import PartitionSpec as P

dz_km = 0.01
dx_km = 0.0125
base_hertz = 3.0
step_hertz = 4.0
taper = 0.5
vmem_bytes = 56 * 1024 * 1024


def split_high_low(value):
    high = lax.reduce_precision(value, 8, 7)
    return high.astype(jnp.bfloat16), (value - high).astype(jnp.bfloat16)


def toeplitz_blocks(length, omega):
    quarter = length // 4
    place = jnp.arange(quarter, dtype=jnp.int32)
    kept = 4 * place[None, :] + jnp.arange(4, dtype=jnp.int32)[:, None]
    signed = jnp.where(kept * 2 < length, kept, kept - length)
    square = (signed.astype(jnp.float32) * (2.0 * math.pi / (length * dx_km))) ** 2
    kmax = math.pi / dx_km
    damp = jnp.exp(-taper * square / (kmax * kmax)) / float(length)
    phase = (-dz_km / omega) * square
    amp_r = (damp * jnp.cos(phase))[:, None, :]
    amp_i = (damp * jnp.sin(phase))[:, None, :]
    turns = (kept[:, None, :] * place[None, :, None] % length).astype(jnp.float32)
    turns = turns * (2.0 * math.pi / length)
    cos_v = jnp.cos(turns)
    sin_v = jnp.sin(turns)
    left = jnp.concatenate([cos_v * amp_r - sin_v * amp_i, sin_v * amp_r + cos_v * amp_i], axis=2)
    right = jnp.concatenate(
        [jnp.concatenate([cos_v, sin_v], axis=2), jnp.concatenate([-sin_v, cos_v], axis=2)], axis=1
    )
    both = jnp.einsum("kbm,kcm->kbc", left, right, precision=lax.Precision.HIGHEST)
    return both[:, :, :quarter], both[:, :, quarter:]


def pack(real, imag, sign):
    top = jnp.concatenate([real, -sign * imag], axis=2)
    low = jnp.concatenate([sign * imag, real], axis=2)
    return split_high_low(jnp.concatenate([top, low], axis=1))


def column_matrix(real, imag):
    return pack(real, imag, 1.0)


def row_matrix(real, imag):
    turned_r = jnp.stack([real[0], real[3], real[2], real[1]])
    turned_i = jnp.stack([imag[0], imag[3], imag[2], imag[1]])
    return pack(turned_r, turned_i, -1.0)


def butterfly(re, im, sign):
    sum_r, dif_r = re[0] + re[2], re[0] - re[2]
    sum_i, dif_i = im[0] + im[2], im[0] - im[2]
    odd_r, gap_r = re[1] + re[3], re[1] - re[3]
    odd_i, gap_i = im[1] + im[3], im[1] - im[3]
    if sign < 0:
        gap_r, gap_i = -gap_r, -gap_i
    out_r = [sum_r + odd_r, dif_r - gap_i, sum_r - odd_r, dif_r + gap_i]
    out_i = [sum_i + odd_i, dif_i + gap_r, sum_i - odd_i, dif_i - gap_r]
    return out_r, out_i


def halves(value):
    high = value.astype(jnp.bfloat16)
    return high, (value - high.astype(jnp.float32)).astype(jnp.bfloat16)


def dot(left, right):
    return jnp.dot(left, right, preferred_element_type=jnp.float32)


def filter_rows(re, im, high_ref, low_ref):
    quarter = re[0].shape[1]
    re, im = butterfly(re, im, -1)
    out_r, out_i = [], []
    for k in range(4):
        high, low = halves(jnp.concatenate([re[k], im[k]], axis=1))
        out = dot(high, high_ref[k]) + (dot(low, high_ref[k]) + dot(high, low_ref[k]))
        out_r.append(out[:, :quarter])
        out_i.append(out[:, quarter:])
    return butterfly(out_r, out_i, 1)


def filter_cols(re, im, high_ref, low_ref):
    quarter = re[0].shape[0]
    re, im = butterfly(re, im, -1)
    out_r, out_i = [], []
    for k in range(4):
        high, low = halves(jnp.concatenate([re[k], im[k]], axis=0))
        out = dot(high_ref[k], high) + (dot(high_ref[k], low) + dot(low_ref[k], high))
        out_r.append(out[:quarter])
        out_i.append(out[quarter:])
    return butterfly(out_r, out_i, 1)


def first_kernel(sign, field_ref, high_ref, low_ref, out_ref):
    quarter = field_ref.shape[3] // 4
    re, im = [], []
    for j in range(4):
        span = pl.ds(j * quarter, quarter)
        re.append(field_ref[0, 0, :, span])
        im.append(sign * field_ref[1, 0, :, span])
    re, im = filter_rows(re, im, high_ref, low_ref)
    for j in range(4):
        out_ref[j, 0] = re[j]
        out_ref[j, 1] = im[j]


def middle_step(cos_ref, sin_ref, field_ref, high_ref, low_ref, out_ref, keep):
    re = [field_ref[j, 0] for j in range(4)]
    im = [field_ref[j, 1] for j in range(4)]
    re, im = filter_cols(re, im, high_ref, low_ref)
    for j in range(4):
        cos_v, sin_v = cos_ref[j], sin_ref[j]
        re[j], im[j] = re[j] * cos_v - im[j] * sin_v, im[j] * cos_v + re[j] * sin_v
        keep(j, re[j], im[j])
    re, im = filter_cols(re, im, high_ref, low_ref)
    for j in range(4):
        out_ref[j, 0] = re[j]
        out_ref[j, 1] = im[j]


def middle_source(cos_ref, sin_ref, field_ref, high_ref, low_ref, out_ref, mid_ref):
    def keep(j, re, im):
        mid_ref[j, 0] = re
        mid_ref[j, 1] = im

    middle_step(cos_ref, sin_ref, field_ref, high_ref, low_ref, out_ref, keep)


def middle_receiver(cos_ref, sin_ref, field_ref, high_ref, low_ref, mid_ref, out_ref, term_ref):
    def keep(j, re, im):
        term_ref[j] = mid_ref[j, 0] * re - mid_ref[j, 1] * im

    middle_step(cos_ref, sin_ref, field_ref, high_ref, low_ref, out_ref, keep)


def last_step(cos_ref, sin_ref, field_ref, high_ref, low_ref, keep):
    quarter = field_ref.shape[3]
    re = [field_ref[j, 0] for j in range(4)]
    im = [field_ref[j, 1] for j in range(4)]
    re, im = filter_rows(re, im, high_ref, low_ref)
    for j in range(4):
        span = pl.ds(j * quarter, quarter)
        cos_v, sin_v = cos_ref[:, span], sin_ref[:, span]
        keep(span, re[j] * cos_v - im[j] * sin_v, im[j] * cos_v + re[j] * sin_v)


def last_source(cos_ref, sin_ref, field_ref, high_ref, low_ref, source_ref):
    def keep(span, re, im):
        source_ref[0, 0, :, span] = re
        source_ref[1, 0, :, span] = im

    last_step(cos_ref, sin_ref, field_ref, high_ref, low_ref, keep)


def last_receiver(cos_ref, sin_ref, field_ref, high_ref, low_ref, source_ref, receiver_ref, term_ref):
    def keep(span, re, im):
        term_ref[span.start // span.size] = (
            source_ref[0, 0, :, span] * re - source_ref[1, 0, :, span] * im
        )
        receiver_ref[0, 0, :, span] = re
        receiver_ref[1, 0, :, span] = -im

    last_step(cos_ref, sin_ref, field_ref, high_ref, low_ref, keep)


def params():
    return pltpu.CompilerParams(vmem_limit_bytes=vmem_bytes, dimension_semantics=("arbitrary",))


def whole(shape):
    return pl.BlockSpec(shape, lambda i: (0,) * len(shape))


def swap(blocks):
    return lax.all_to_all(blocks, "row", split_axis=0, concat_axis=0, tiled=True)


def sum_strips(strips):
    count = strips.shape[0]
    me = lax.axis_index("freq")
    total = lax.dynamic_index_in_dim(strips, me, 0, keepdims=False)
    for shift in range(1, count):
        sent = lax.dynamic_index_in_dim(strips, (me + shift) % count, 0, keepdims=False)
        total = total + lax.ppermute(sent, "freq", [(i, (i + shift) % count) for i in range(count)])
    return total


def body(source_field, receiver_field, slowness, owner, freq_index):
    rows, width = source_field.shape[2:]
    row_count = lax.axis_size("row")
    freq_count = lax.axis_size("freq")
    height = rows * row_count
    cols = width // row_count
    quart_w = width // 4
    quart_h = height // 4
    more = row_count // 4
    omega = 2.0 * math.pi * (base_hertz + step_hertz * freq_index.astype(jnp.float32))

    def turning(slab):
        theta = slab * (omega[0] * dz_km)
        return jnp.cos(theta), jnp.sin(theta)

    def owned(depth):
        return jnp.where(lax.axis_index("freq") == owner[depth], slowness[0], 0.0)

    turned = swap(jnp.moveaxis(owned(0).reshape(rows, row_count, cols), 1, 0))
    piece_last = lax.psum_scatter(owned(1), "freq", scatter_dimension=0, tiled=True)
    source_field, turned = lax.optimization_barrier((source_field, turned))
    piece = lax.psum_scatter(turned, "freq", scatter_dimension=0, tiled=True)
    receiver_field, piece = lax.optimization_barrier((receiver_field, piece))
    slab_first = lax.all_gather(piece, "freq", axis=0, tiled=True)
    piece_last, slab_first = lax.optimization_barrier((piece_last, slab_first))
    slab_last = lax.all_gather(piece_last, "freq", axis=0, tiled=True)
    turn_first = turning(slab_first.reshape(4, quart_h, cols))

    block_w = toeplitz_blocks(width, omega[0])
    block_h = block_w if height == width else toeplitz_blocks(height, omega[0])
    row_high, row_low = row_matrix(*block_w)
    col_high, col_low = column_matrix(*block_h)
    mat_w = whole((4, 2 * quart_w, 2 * quart_w))
    mat_h = whole((4, 2 * quart_h, 2 * quart_h))

    step = min(rows, 128)
    row_block = pl.BlockSpec((2, 1, step, width), lambda i: (0, 0, i, 0))
    quarter_block = pl.BlockSpec((4, 2, step, quart_w), lambda i: (0, 0, i, 0))
    line_block = pl.BlockSpec((step, width), lambda i: (i, 0))
    col_block = pl.BlockSpec((4, 2, quart_h, cols), lambda i: (0, 0, 0, 0))
    term_block = pl.BlockSpec((4, quart_h, cols), lambda i: (0, 0, 0))
    quarter_shape = jax.ShapeDtypeStruct((4, 2, rows, quart_w), jnp.float32)
    col_shape = jax.ShapeDtypeStruct((4, 2, quart_h, cols), jnp.float32)
    term_shape = jax.ShapeDtypeStruct((4, quart_h, cols), jnp.float32)
    strip_block = pl.BlockSpec((4, step, quart_w), lambda i: (0, i, 0))
    strip_shape = jax.ShapeDtypeStruct((4, rows, quart_w), jnp.float32)
    field_shape = jax.ShapeDtypeStruct(source_field.shape, jnp.float32)

    def first(field, sign):
        return pl.pallas_call(
            partial(first_kernel, sign),
            grid=(rows // step,),
            in_specs=[row_block, mat_w, mat_w],
            out_specs=quarter_block,
            out_shape=quarter_shape,
            compiler_params=params(),
        )(field, row_high, row_low)

    def to_cols(fields):
        if more > 1:
            fields = fields.reshape(4, 2, rows, more, cols)
            fields = jnp.moveaxis(fields, 3, 1).reshape(row_count, 2, rows, cols)
        fields = swap(fields)
        if more > 1:
            fields = fields.reshape(4, more, 2, rows, cols)
            fields = jnp.moveaxis(fields, 1, 2).reshape(4, 2, quart_h, cols)
        return fields

    def to_rows(fields):
        if more > 1:
            fields = fields.reshape(4, 2, more, rows, cols)
            fields = jnp.moveaxis(fields, 2, 1).reshape(row_count, 2, rows, cols)
        fields = swap(fields)
        if more > 1:
            fields = fields.reshape(4, more, 2, rows, cols)
            fields = jnp.moveaxis(fields, 1, 3).reshape(4, 2, rows, quart_w)
        return fields

    source = to_cols(first(source_field, 1.0))
    receiver = to_cols(first(receiver_field, -1.0))
    source, middle = pl.pallas_call(
        middle_source,
        grid=(1,),
        in_specs=[term_block, term_block, col_block, mat_h, mat_h],
        out_specs=[col_block, col_block],
        out_shape=[col_shape, col_shape],
        compiler_params=params(),
    )(*turn_first, source, col_high, col_low)
    source = to_rows(source)
    receiver, term = pl.pallas_call(
        middle_receiver,
        grid=(1,),
        in_specs=[term_block, term_block, col_block, mat_h, mat_h, col_block],
        out_specs=[col_block, term_block],
        out_shape=[col_shape, term_shape],
        compiler_params=params(),
    )(*turn_first, receiver, col_high, col_low, middle)
    receiver, term, slab_last = lax.optimization_barrier((receiver, term, slab_last))
    turn_last = turning(slab_last)
    receiver = to_rows(receiver)

    term = term.reshape(height, cols)
    if row_count == freq_count:
        part = lax.psum_scatter(term, "freq", scatter_dimension=0, tiled=True)
        pairs = [
            (r * freq_count + f, f * freq_count + r)
            for r in range(row_count)
            for f in range(freq_count)
        ]
        image_first = lax.ppermute(part, ("row", "freq"), pairs)
    else:
        term = lax.all_to_all(term, "row", split_axis=0, concat_axis=1, tiled=True)
        image_first = lax.psum_scatter(term, "freq", scatter_dimension=1, tiled=True)

    source_out = pl.pallas_call(
        last_source,
        grid=(rows // step,),
        in_specs=[line_block, line_block, quarter_block, mat_w, mat_w],
        out_specs=row_block,
        out_shape=field_shape,
        compiler_params=params(),
    )(*turn_last, source, row_high, row_low)
    receiver_out, term = pl.pallas_call(
        last_receiver,
        grid=(rows // step,),
        in_specs=[line_block, line_block, quarter_block, mat_w, mat_w, row_block],
        out_specs=[row_block, strip_block],
        out_shape=[field_shape, strip_shape],
        compiler_params=params(),
    )(*turn_last, receiver, row_high, row_low, source_out)
    if freq_count == 4:
        image_last = sum_strips(term)
    else:
        term = jnp.moveaxis(term, 0, 1).reshape(rows, width)
        image_last = lax.psum_scatter(term, "freq", scatter_dimension=1, tiled=True)
    return source_out, receiver_out, jnp.stack([image_first, image_last])


def solution(mesh):
    in_specs = (
        P(None, ("shot", "freq"), "row", None),
        P(None, ("shot", "freq"), "row", None),
        P("freq", "row", None),
        P(),
        P(("shot", "freq")),
    )
    out_specs = (
        P(None, ("shot", "freq"), "row", None),
        P(None, ("shot", "freq"), "row", None),
        P("shot", "row", "freq"),
    )
    return jax.shard_map(body, mesh=mesh, in_specs=in_specs, out_specs=out_specs, check_vma=False)
```
